32 devices in a mesh: groups: 2 (over y), slab: 4 (over z), sub: 4 (over x, core).
Axes of the slice: x: 2, y: 2, z: 4, core: 2. Of those that a mesh axis runs over, the one named last changes fastest.
Arguments:
- image: bfloat16 [2, 32, 128, 128], P(None, ('groups', 'slab', 'sub')), parts along dimension 1, may hold values from -6 to 6
- w_in: bfloat16 [9, 32, 2], replicated, may hold values from -2 to 2
- w_down2: bfloat16 [9, 64, 32], replicated, may hold values from -0.5 to 0.5
- w_down3: bfloat16 [9, 128, 64], replicated, may hold values from -0.375 to 0.375
- w_up3: bfloat16 [9, 64, 128], replicated, may hold values from -0.25 to 0.25
- w_up2: bfloat16 [9, 32, 64], replicated, may hold values from -0.375 to 0.375
- w_up1: bfloat16 [9, 32, 32], replicated, may hold values from -0.5 to 0.5
- w_out: bfloat16 [3, 32], replicated, may hold values from -1 to 1
Outputs:
- flows: float32 [4, 32, 128, 128], P(None, ('groups', 'slab', 'sub')), parts along dimension 1
The draws below stay inside these ranges and needn't reach their ends.
There are 2 independent parts, one for each index of `groups`. The reference program is written for one: setup_inputs(seed, part) draws one part's arguments, and reference() takes and returns one part's arrays. A program takes and returns all parts, laid end to end along the dimension named above; an argument that names none is the same for every part. Nothing has to cross between parts.
All inputs are finite; a program needn't handle non-finite values.
Results may differ from the reference program's by a relative error of at most 0.024.
Values may be sent and summed in bfloat16 or wider, within the bound.
A program may use at most 128 MiB of HBM per device.

```python
import jax
import jax.numpy as jnp
from jax import lax

C_IN = 2
C1 = 32
C2 = 64
C3 = 128
SIDE = 128
NZ = 16


def block_scale(rng, dims, cuts, smallest, top_value):
    loudness = 1.0
    for dim, shards_of in cuts:
        heights = jax.random.uniform(jax.random.fold_in(jax.random.fold_in(rng, 6), dim), (shards_of,), jnp.float32, smallest / len(cuts), top_value / len(cuts))
        loudness = loudness * jnp.repeat(jnp.exp(heights), dims[dim] // shards_of).reshape((-1,) + (1,) * (len(dims) - 1 - dim))
    return loudness


def centred(rng, shape, deviation, reach, shards=(), held_as=jnp.bfloat16):
    drawn = deviation * jax.random.normal(rng, shape, jnp.float32)
    if shards:
        drawn = drawn * block_scale(rng, shape, shards, -0.22, 0.18)
    return jnp.clip(drawn, -reach, reach).astype(held_as)


def setup_inputs(seed: int = 0, part: int = 0) -> dict:
    splits = jax.random.split(jax.random.key(seed), 9)
    part_splits = jax.random.split(jax.random.fold_in(splits[8], part), 9)
    return {
        "image": centred(part_splits[0], (C_IN, NZ, SIDE, SIDE), 1.0, 6.0, ((1, 16),)),
        "w_in": centred(splits[1], (9, C1, C_IN), (9 * C_IN // 2) ** -0.5, 2.0),
        "w_down2": centred(splits[2], (9, C2, C1), (9 * C1 // 2) ** -0.5, 0.5),
        "w_down3": centred(splits[3], (9, C3, C2), (9 * C2 // 2) ** -0.5, 0.375),
        "w_up3": centred(splits[4], (9, C2, C3), (9 * C3 // 2) ** -0.5, 0.25),
        "w_up2": centred(splits[5], (9, C1, C2), (9 * C2 // 2) ** -0.5, 0.375),
        "w_up1": centred(splits[6], (9, C1, C1), (9 * C1 // 2) ** -0.5, 0.5),
        "w_out": centred(splits[7], (3, C1), C1 ** -0.5, 1.0),
    }


def conv_three(values, kernel):
    height, span = values.shape[2], values.shape[3]
    padded = jnp.pad(values.astype(jnp.float32), ((0, 0), (0, 0), (1, 1), (1, 1)))
    summed = jnp.zeros((values.shape[0], kernel.shape[1], height, span), jnp.float32)
    for kernel_tap in range(9):
        down_off = kernel_tap // 3
        right_off = kernel_tap % 3
        window = padded[:, :, down_off:down_off + height, right_off:right_off + span]
        summed = summed + jnp.einsum("oc,bchw->bohw", kernel[kernel_tap].astype(jnp.float32), window)
    return summed


def relu_round(values):
    return jnp.maximum(values, 0.0).astype(jnp.bfloat16)


def pool_half(values):
    count, chan_num, height, span = values.shape
    blocks = values.astype(jnp.float32).reshape(count, chan_num, height // 2, 2, span // 2, 2)
    return jnp.mean(blocks, axis=(3, 5)).astype(jnp.bfloat16)


def upsample(values):
    return jnp.repeat(jnp.repeat(values, 2, axis=2), 2, axis=3)


def run_unet(slices, weights):
    w_in, w_down2, w_down3, w_up3, w_up2, w_up1, w_out = weights
    level_one = relu_round(conv_three(slices, w_in))
    level_two = relu_round(conv_three(pool_half(level_one), w_down2))
    level_three = relu_round(conv_three(pool_half(level_two), w_down3))
    decoded_three = relu_round(conv_three(level_three, w_up3))
    skip_two = (upsample(decoded_three).astype(jnp.float32) + level_two.astype(jnp.float32)).astype(jnp.bfloat16)
    decoded_two = relu_round(conv_three(skip_two, w_up2))
    skip_one = (upsample(decoded_two).astype(jnp.float32) + level_one.astype(jnp.float32)).astype(jnp.bfloat16)
    decoded_one = relu_round(conv_three(skip_one, w_up1))
    return jnp.einsum("oc,bchw->bohw", w_out.astype(jnp.float32), decoded_one.astype(jnp.float32))


def run_blocks(slices, weights):
    count = slices.shape[0]
    grouped = slices.reshape((count // 8, 8) + slices.shape[1:])
    result = lax.map(lambda block_in: run_unet(block_in, weights), grouped)
    return result.reshape((count,) + result.shape[2:])


def reference(image, w_in, w_down2, w_down3, w_up3, w_up2, w_up1, w_out):
    weights = (w_in, w_down2, w_down3, w_up3, w_up2, w_up1, w_out)
    flows_xy = jnp.transpose(run_blocks(jnp.transpose(image, (1, 0, 2, 3)), weights), (1, 0, 2, 3))
    flows_xz = jnp.transpose(run_blocks(jnp.transpose(image, (2, 0, 1, 3)), weights), (1, 2, 0, 3))
    flows_yz = jnp.transpose(run_blocks(jnp.transpose(image, (3, 0, 1, 2)), weights), (1, 2, 3, 0))
    flow_z = (flows_xz[0] + flows_yz[0]) * 0.5
    flow_y = (flows_xy[0] + flows_yz[1]) * 0.5
    flow_x = (flows_xy[1] + flows_xz[1]) * 0.5
    probability = (flows_xy[2] + flows_xz[2] + flows_yz[2]) / 3.0
    return jnp.stack([flow_z, flow_y, flow_x, probability], axis=0)
```

```python
import functools

import jax
import jax.numpy as jnp
from jax import lax
from jax.experimental import pallas as pl
from jax.experimental.pallas import tpu as pltpu
from jax.sharding import PartitionSpec as P

F32, BF16 = jnp.float32, jnp.bfloat16
BLOCKS = 16
LANES = 256
AXES = ("slab", "sub")

BANDS = {
    "down2": (32, 64, (0, 0, 1, 1, 2, 2, 3, 3, 4, 4, -1, -1), 0.25),
    "down3": (64, 128, (0, 0, 1, 1, 2, 2, -1, -1), 0.25),
    "up3": (128, 128, (0, 1, 2, -1), 1.0),
    "up2": (64, 64, (0, 1, 2, 3, 4, -1), 1.0),
    "up1": (32, 32, (0, 1, 2, 3, 4, 5, 6, 7, 8, None, None, -1), 1.0),
}


def tile_weights(weight, chan_in):
    flipped = jnp.swapaxes(weight, 1, 2)
    return jnp.tile(flipped, (1, 1, LANES // weight.shape[1]))


def build_band(name, tiled_ref, band_ref):
    chan, cell_lanes, cells, scale = BANDS[name]
    cell_of_lane = lax.broadcasted_iota(jnp.int32, (chan, LANES), 1) // cell_lanes
    depth = chan * len(cells)
    for down in range(3):
        taps = [tiled_ref[3 * down + c].astype(F32) * scale for c in range(3)]
        for number, cell in enumerate(cells):
            total = jnp.zeros((chan, LANES), F32)
            if cell is not None:
                for c in range(3):
                    total = jnp.where(cell_of_lane == cell - c + 1, taps[c], total)
            start = down * depth + number * chan
            band_ref[start : start + chan, :] = total.astype(BF16)


def build_in(tiled_ref, band_ref):
    shape = (128, LANES)
    row = lax.broadcasted_iota(jnp.int32, shape, 0)
    cell = lax.broadcasted_iota(jnp.int32, shape, 1) // 32
    tiled = tiled_ref[...].astype(F32)
    for down in range(3):
        total = jnp.zeros(shape, F32)
        for chan in range(2):
            for c in range(3):
                index = (3 * down + c) * 2 + chan
                total = jnp.where(row - 16 * chan - cell == c, tiled[index : index + 1, :], total)
        band_ref[128 * down : 128 * down + 128, :] = total.astype(BF16)


def build_out(tiled_ref, band_ref):
    shape = (LANES, 128)
    keep = lax.broadcasted_iota(jnp.int32, shape, 0) // 32 == lax.broadcasted_iota(
        jnp.int32, shape, 1
    ) % 8
    for out in range(3):
        value = tiled_ref[:, out : out + 1].astype(F32)
        band_ref[:, 128 * out : 128 * out + 128] = jnp.where(keep, value, 0.0).astype(BF16)


def neighbours(values):
    count = values.shape[0]
    block = lax.broadcasted_iota(jnp.int32, (count, BLOCKS, 128), 1)
    right = pltpu.roll(values[..., :128], 1, 1)
    left = pltpu.roll(values[..., 128:], BLOCKS - 1, 1)
    right = jnp.where(block == 0, 0.0, right)
    left = jnp.where(block == BLOCKS - 1, 0.0, left)
    return right, left


def narrow_halo(values):
    right, left = neighbours(values)
    lane = lax.broadcasted_iota(jnp.int32, right.shape, 2)
    return jnp.where(lane < 64, right, left)


def store_narrow(ref, start, values):
    count = values.shape[0]
    ref[pl.ds(start, count), :, :256] = values.astype(BF16)
    ref[pl.ds(start, count), :, 256:] = narrow_halo(values).astype(BF16)


def store_wide(ref, start, values):
    count = values.shape[0]
    right, left = neighbours(values)
    ref[pl.ds(start, count), :, :256] = values.astype(BF16)
    ref[pl.ds(start, count), :, 256:384] = right.astype(BF16)
    ref[pl.ds(start, count), :, 384:] = left.astype(BF16)


def conv(ref, band_ref, start, count, span):
    depth = ref.shape[2]
    parts = [ref[pl.ds(start + down * span, count)] for down in range(3)]
    rows = jnp.concatenate(parts, axis=-1).reshape(count * BLOCKS, 3 * depth)
    total = jnp.dot(rows, band_ref[...], preferred_element_type=F32)
    return jnp.maximum(total, 0.0).reshape(count, BLOCKS, LANES)


def pair_sum(values, span):
    count = values.shape[0]
    pairs = values.reshape(count // (2 * span), 2, span, BLOCKS, LANES)
    return (pairs[:, 0] + pairs[:, 1]).reshape(count // 2, BLOCKS, LANES)


def twice(values, span):
    count = values.shape[0]
    rows = values.reshape(count // span, 1, span, BLOCKS, LANES)
    return jnp.broadcast_to(rows, (count // span, 2, span, BLOCKS, LANES)).reshape(
        2 * count, BLOCKS, LANES
    )


def clear_edges(ref, height, span):
    zero = jnp.zeros((span,) + tuple(ref.shape[1:]), ref.dtype)
    ref[pl.ds(0, span)] = zero
    ref[pl.ds((height + 1) * span, span)] = zero


def chunks(total, count, body):
    steps = total // count
    if steps == 1:
        body(0)
    else:

        def step(i, carry):
            body(i * count)
            return carry

        lax.fori_loop(0, steps, step, 0)


def unet(height, span, load, emit, bands, scratch):
    b_in, b_down2, b_down3, b_up3, b_up2, b_up1, b_out = bands
    win, a1, p1, a2, p2, a3, s2, s1 = scratch
    for ref, rows in ((win, height), (p1, height // 2), (p2, height // 4), (a3, height // 4)):
        clear_edges(ref, rows, span)
    clear_edges(s2, height // 2, span)
    clear_edges(s1, height, span)
    units = height * span
    count = max(32, 2 * span)

    def fill(g):
        shape = (count, BLOCKS, 128)
        lane = lax.broadcasted_iota(jnp.int32, shape, 2)
        block = lax.broadcasted_iota(jnp.int32, shape, 1)
        outside = ((block == BLOCKS - 1) & (lane % 16 == 0)) | ((block == 0) & (lane % 16 == 9))
        rolled = []
        for chan in range(2):
            row = pltpu.roll(load(chan, g, count).astype(F32), 9 + 16 * chan, 1)
            row = jnp.broadcast_to(row[:, None, :], shape)
            rolled.append(pltpu.roll(row, 0, 2, stride=8, stride_axis=1))
        merged = jnp.where(lane < 16, rolled[0], rolled[1])
        win[pl.ds(g + span, count)] = jnp.where(outside, 0.0, merged).astype(BF16)

    chunks(units, count, fill)

    def level1(g):
        values = conv(win, b_in, g, count, span)
        a1[pl.ds(g, count)] = values.astype(BF16)
        store_narrow(p1, g // 2 + span, pair_sum(values, span))

    chunks(units, count, level1)

    def level2(g):
        values = conv(p1, b_down2, g, count, span)
        a2[pl.ds(g, count)] = values.astype(BF16)
        store_wide(p2, g // 2 + span, pair_sum(values, span))

    chunks(units // 2, count, level2)

    def level3(g):
        store_wide(a3, g + span, conv(p2, b_down3, g, count, span))

    chunks(units // 4, count, level3)

    def level3_up(g):
        values = twice(conv(a3, b_up3, g, count, span), span)
        skip = a2[pl.ds(2 * g, 2 * count)].astype(F32)
        store_narrow(s2, 2 * g + span, values + skip)

    chunks(units // 4, count, level3_up)

    def level2_up(g):
        values = twice(conv(s2, b_up2, g, count, span), span)
        skip = a1[pl.ds(2 * g, 2 * count)].astype(F32)
        store_narrow(s1, 2 * g + span, values + skip)

    chunks(units // 2, count, level2_up)

    def level1_up(g):
        values = conv(s1, b_up1, g, count, span).astype(BF16)
        spread = jnp.dot(
            values.reshape(count * BLOCKS, LANES), b_out[...], preferred_element_type=F32
        ).reshape(count, BLOCKS, 384)
        shape = (count, BLOCKS, 384)
        lane = lax.broadcasted_iota(jnp.int32, shape, 2)
        block = lax.broadcasted_iota(jnp.int32, shape, 1)
        emit(g, jnp.sum(jnp.where(lane % 128 // 8 == BLOCKS - 1 - block, spread, 0.0), axis=1))

    chunks(units, count, level1_up)


def unit_scratch(height, span):
    def spec(rows, lanes, edge=True):
        return pltpu.VMEM(((rows + (2 if edge else 0)) * span, BLOCKS, lanes), BF16)

    return [
        spec(height, 128),
        spec(height, 256, False),
        spec(height // 2, 384),
        spec(height // 2, 256, False),
        spec(height // 4, 512),
        spec(height // 4, 512),
        spec(height // 2, 384),
        spec(height, 384),
    ]


BAND_SCRATCH = [
    pltpu.VMEM((384, 256), BF16),
    pltpu.VMEM((1152, 256), BF16),
    pltpu.VMEM((1536, 256), BF16),
    pltpu.VMEM((1536, 256), BF16),
    pltpu.VMEM((1152, 256), BF16),
    pltpu.VMEM((1152, 256), BF16),
    pltpu.VMEM((256, 384), BF16),
]


def build_all(tiled, bands):
    build_in(tiled[0], bands[0])
    for name, source, band in zip(("down2", "down3", "up3", "up2", "up1"), tiled[1:6], bands[1:6]):
        build_band(name, source, band)
    build_out(tiled[6], bands[6])


def net_kernel(height, span, x_ref, *refs):
    tiled, out_ref, bands, scratch = refs[:7], refs[7], refs[8:15], refs[15:]
    build_all(tiled, bands)

    def load(chan, start, count):
        return x_ref[chan, pl.ds(pl.multiple_of(start, 16), count), :]

    def emit(start, values):
        count = values.shape[0]
        out_ref[pl.ds(pl.multiple_of(start, 16), count), :] = values.astype(out_ref.dtype)

    unet(height, span, load, emit, bands, scratch)


def run_net(x, tiled, height, span, dtype):
    return pl.pallas_call(
        functools.partial(net_kernel, height, span),
        out_shape=jax.ShapeDtypeStruct((height * span, 384), dtype),
        in_specs=[pl.BlockSpec(memory_space=pltpu.VMEM)] * 8,
        out_specs=pl.BlockSpec(memory_space=pltpu.VMEM),
        scratch_shapes=BAND_SCRATCH + unit_scratch(height, span),
        compiler_params=pltpu.CompilerParams(vmem_limit_bytes=48 << 20),
    )(x, *tiled)


def prepare(weights):
    w_in, w_out = weights[0], weights[6]
    tiled_in = jnp.tile(jnp.swapaxes(w_in, 1, 2).reshape(18, 32), (1, 8))
    tiled_out = jnp.tile(jnp.swapaxes(w_out, 0, 1), (8, 1))
    return [tiled_in] + [tile_weights(w, w.shape[2]) for w in weights[1:6]] + [tiled_out]


def shards(image, *weights):
    tiled = prepare(weights)
    chan, _, extent, _ = image.shape
    plane = image[:, 0]
    peers = lax.axis_size(AXES)
    cut = extent // peers
    both = jnp.stack([plane, jnp.swapaxes(plane, 1, 2)])
    send = jnp.transpose(both.reshape(2, chan, peers, cut, extent), (2, 1, 0, 3, 4))
    got = lax.all_to_all(send, AXES, split_axis=0, concat_axis=0, tiled=True)
    cross = jnp.transpose(got, (1, 0, 2, 3, 4)).reshape(chan, peers * 2 * cut, extent)
    flat = run_net(plane, tiled, extent, 1, F32).reshape(extent, 3, extent)
    result = run_net(cross, tiled, peers, 2 * cut, BF16).reshape(peers, 2, cut, 3, extent)
    back = lax.all_to_all(result, AXES, split_axis=0, concat_axis=0, tiled=True)
    back = jnp.transpose(back, (1, 3, 0, 2, 4)).reshape(2, 3, extent, extent).astype(F32)
    xz = back[0]
    yz = jnp.swapaxes(back[1], 1, 2)
    flow_z = (xz[0] + yz[0]) * 0.5
    flow_y = (flat[:, 0] + yz[1]) * 0.5
    flow_x = (flat[:, 1] + xz[1]) * 0.5
    prob = (flat[:, 2] + xz[2] + yz[2]) / 3.0
    return jnp.stack([flow_z, flow_y, flow_x, prob])[:, None]


def solution(mesh):
    split = P(None, ("groups", "slab", "sub"), None, None)
    return jax.shard_map(
        shards,
        mesh=mesh,
        in_specs=(split,) + (P(),) * 7,
        out_specs=split,
        check_vma=False,
    )
```

```python
import functools

import jax
import jax.numpy as jnp
from jax import lax
from jax.experimental import pallas as pl
from jax.experimental.pallas import tpu as pltpu
from jax.sharding import PartitionSpec as P

F32, BF16 = jnp.float32, jnp.bfloat16
BLOCKS = 16
LANES = 256
AXES = ("slab", "sub")

BANDS = {
    "down2": (32, 64, (0, 0, 1, 1, 2, 2, 3, 3, 4, 4, -1, -1), 0.25),
    "down3": (64, 128, (0, 0, 1, 1, 2, 2, -1, -1), 0.25),
    "up3": (128, 128, (0, 1, 2, -1), 1.0),
    "up2": (64, 64, (0, 1, 2, 3, 4, -1), 1.0),
    "up1": (32, 32, (0, 1, 2, 3, 4, 5, 6, 7, 8, None, None, -1), 1.0),
}


def build_band(name, weight_ref, band_ref):
    chan, cell_lanes, cells, scale = BANDS[name]
    cell_of_lane = lax.broadcasted_iota(jnp.int32, (chan, LANES), 1) // cell_lanes
    depth = chan * len(cells)
    chan_out = weight_ref.shape[1]
    for down in range(3):
        taps = []
        for c in range(3):
            flipped = (weight_ref[3 * down + c].astype(F32) * scale).T
            taps.append(jnp.concatenate([flipped] * (LANES // chan_out), axis=1))
        for number, cell in enumerate(cells):
            total = jnp.zeros((chan, LANES), F32)
            if cell is not None:
                for c in range(3):
                    total = jnp.where(cell_of_lane == cell - c + 1, taps[c], total)
            start = down * depth + number * chan
            band_ref[start : start + chan, :] = total.astype(BF16)


def build_in(tiled_ref, band_ref):
    shape = (128, LANES)
    row = lax.broadcasted_iota(jnp.int32, shape, 0)
    cell = lax.broadcasted_iota(jnp.int32, shape, 1) // 32
    tiled = tiled_ref[...].astype(F32)
    for down in range(3):
        total = jnp.zeros(shape, F32)
        for chan in range(2):
            for c in range(3):
                index = (3 * down + c) * 2 + chan
                total = jnp.where(row - 16 * chan - cell == c, tiled[index : index + 1, :], total)
        band_ref[128 * down : 128 * down + 128, :] = total.astype(BF16)


def build_out(tiled_ref, band_ref):
    shape = (LANES, 128)
    keep = lax.broadcasted_iota(jnp.int32, shape, 0) // 32 == lax.broadcasted_iota(
        jnp.int32, shape, 1
    ) % 8
    for out in range(3):
        value = tiled_ref[:, out : out + 1].astype(F32)
        band_ref[:, 128 * out : 128 * out + 128] = jnp.where(keep, value, 0.0).astype(BF16)


def neighbours(values):
    count = values.shape[0]
    block = lax.broadcasted_iota(jnp.int32, (count, BLOCKS, 128), 1)
    right = pltpu.roll(values[..., :128], 1, 1)
    left = pltpu.roll(values[..., 128:], BLOCKS - 1, 1)
    right = jnp.where(block == 0, 0.0, right)
    left = jnp.where(block == BLOCKS - 1, 0.0, left)
    return right, left


def narrow_halo(values):
    right, left = neighbours(values)
    lane = lax.broadcasted_iota(jnp.int32, right.shape, 2)
    return jnp.where(lane < 64, right, left)


def store_narrow(ref, start, values):
    count = values.shape[0]
    ref[pl.ds(start, count), :, :256] = values.astype(BF16)
    ref[pl.ds(start, count), :, 256:] = narrow_halo(values).astype(BF16)


def store_wide(ref, start, values):
    count = values.shape[0]
    right, left = neighbours(values)
    ref[pl.ds(start, count), :, :256] = values.astype(BF16)
    ref[pl.ds(start, count), :, 256:384] = right.astype(BF16)
    ref[pl.ds(start, count), :, 384:] = left.astype(BF16)


def conv(ref, band_ref, start, count, span):
    depth = ref.shape[2]
    parts = [ref[pl.ds(start + down * span, count)] for down in range(3)]
    rows = jnp.concatenate(parts, axis=-1).reshape(count * BLOCKS, 3 * depth)
    total = jnp.dot(rows, band_ref[...], preferred_element_type=F32)
    return jnp.maximum(total, 0.0).reshape(count, BLOCKS, LANES)


def pair_sum(values, span):
    count = values.shape[0]
    pairs = values.reshape(count // (2 * span), 2, span, BLOCKS, LANES)
    return (pairs[:, 0] + pairs[:, 1]).reshape(count // 2, BLOCKS, LANES)


def twice(values, span):
    count = values.shape[0]
    rows = values.reshape(count // span, 1, span, BLOCKS, LANES)
    return jnp.broadcast_to(rows, (count // span, 2, span, BLOCKS, LANES)).reshape(
        2 * count, BLOCKS, LANES
    )


def clear_edges(ref, height, span):
    zero = jnp.zeros((span,) + tuple(ref.shape[1:]), ref.dtype)
    ref[pl.ds(0, span)] = zero
    ref[pl.ds((height + 1) * span, span)] = zero


def chunks(total, count, body, first=0):
    steps = total // count
    if steps == 1:
        body(0)
    else:

        def step(i, carry):
            body(lax.rem(i + first, steps) * count)
            return carry

        lax.fori_loop(0, steps, step, 0)


def unet(height, span, load, emit, bands, scratch, first=0):
    b_in, b_down2, b_down3, b_up3, b_up2, b_up1, b_out = bands
    win, a1, p1, a2, p2, a3, s2, s1 = scratch
    for ref, rows in ((win, height), (p1, height // 2), (p2, height // 4), (a3, height // 4)):
        clear_edges(ref, rows, span)
    clear_edges(s2, height // 2, span)
    clear_edges(s1, height, span)
    units = height * span
    count = max(32, 2 * span)

    def fill(g):
        shape = (count, BLOCKS, 128)
        lane = lax.broadcasted_iota(jnp.int32, shape, 2)
        block = lax.broadcasted_iota(jnp.int32, shape, 1)
        outside = ((block == BLOCKS - 1) & (lane % 16 == 0)) | ((block == 0) & (lane % 16 == 9))
        rolled = []
        for chan in range(2):
            row = pltpu.roll(load(chan, g, count).astype(F32), 9 + 16 * chan, 1)
            row = jnp.broadcast_to(row[:, None, :], shape)
            rolled.append(pltpu.roll(row, 0, 2, stride=8, stride_axis=1))
        merged = jnp.where(lane < 16, rolled[0], rolled[1])
        win[pl.ds(g + span, count)] = jnp.where(outside, 0.0, merged).astype(BF16)

    chunks(units, count, fill)

    def level1(g):
        values = conv(win, b_in, g, count, span)
        a1[pl.ds(g, count)] = values.astype(BF16)
        store_narrow(p1, g // 2 + span, pair_sum(values, span))

    chunks(units, count, level1)

    def level2(g):
        values = conv(p1, b_down2, g, count, span)
        a2[pl.ds(g, count)] = values.astype(BF16)
        store_wide(p2, g // 2 + span, pair_sum(values, span))

    chunks(units // 2, count, level2)

    def level3(g):
        store_wide(a3, g + span, conv(p2, b_down3, g, count, span))

    chunks(units // 4, count, level3)

    def level3_up(g):
        values = twice(conv(a3, b_up3, g, count, span), span)
        skip = a2[pl.ds(2 * g, 2 * count)].astype(F32)
        store_narrow(s2, 2 * g + span, values + skip)

    chunks(units // 4, count, level3_up)

    def level2_up(g):
        values = twice(conv(s2, b_up2, g, count, span), span)
        skip = a1[pl.ds(2 * g, 2 * count)].astype(F32)
        store_narrow(s1, 2 * g + span, values + skip)

    chunks(units // 2, count, level2_up)

    def level1_up(g):
        values = conv(s1, b_up1, g, count, span).astype(BF16)
        spread = jnp.dot(
            values.reshape(count * BLOCKS, LANES), b_out[...], preferred_element_type=F32
        ).reshape(count, BLOCKS, 384)
        shape = (count, BLOCKS, 384)
        lane = lax.broadcasted_iota(jnp.int32, shape, 2)
        block = lax.broadcasted_iota(jnp.int32, shape, 1)
        emit(g, jnp.sum(jnp.where(lane % 128 // 8 == BLOCKS - 1 - block, spread, 0.0), axis=1))

    chunks(units, count, level1_up, first)


def unit_scratch(height, span, extent):
    def spec(rows, lanes, edge=True):
        pad = 2 if edge else 0
        flat = extent * rows // height + pad
        return pltpu.VMEM((max((rows + pad) * span, flat), BLOCKS, lanes), BF16)

    return [
        spec(height, 128),
        spec(height, 256, False),
        spec(height // 2, 384),
        spec(height // 2, 256, False),
        spec(height // 4, 512),
        spec(height // 4, 512),
        spec(height // 2, 384),
        spec(height, 384),
    ]


BAND_SCRATCH = [
    pltpu.VMEM((384, 256), BF16),
    pltpu.VMEM((1152, 256), BF16),
    pltpu.VMEM((1536, 256), BF16),
    pltpu.VMEM((1536, 256), BF16),
    pltpu.VMEM((1152, 256), BF16),
    pltpu.VMEM((1152, 256), BF16),
    pltpu.VMEM((256, 384), BF16),
]


def build_all(tiled, bands):
    build_in(tiled[0], bands[0])
    for name, source, band in zip(("down2", "down3", "up3", "up2", "up1"), tiled[1:6], bands[1:6]):
        build_band(name, source, band)
    build_out(tiled[6], bands[6])


def peer_id(index, inner):
    return {"slab": index // inner, "sub": lax.rem(index, inner)}


def window_kernel(peers, inner, plane_ref, *refs):
    tiled, out_ref, bands = refs[:7], refs[7], refs[8:15]
    scratch = refs[15:23]
    send, recv, flat, back_send, back, out_sem, in_sem, back_out_sem, back_in_sem = refs[23:]
    extent = plane_ref.shape[1]
    cut = extent // peers
    span = 2 * cut
    me = lax.axis_index("slab") * inner + lax.axis_index("sub")

    barrier = pltpu.get_barrier_semaphore()

    def greet(k, carry):
        pl.semaphore_signal(
            barrier,
            inc=1,
            device_id=peer_id(lax.rem(me + k, peers), inner),
            device_id_type=pl.DeviceIdType.MESH,
        )
        return carry

    lax.fori_loop(1, peers, greet, 0)
    for chan in range(2):
        plane = plane_ref[chan].astype(F32)
        send[:, 0, chan] = plane.reshape(peers, cut, extent)
        send[:, 1, chan] = plane.T.reshape(peers, cut, extent)
    recv[pl.ds(me, 1)] = send[pl.ds(me, 1)]
    pl.semaphore_wait(barrier, peers - 1)

    def input_copy(k):
        peer = lax.rem(me + k, peers)
        return pltpu.make_async_remote_copy(
            src_ref=send.at[peer],
            dst_ref=recv.at[me],
            send_sem=out_sem.at[k],
            recv_sem=in_sem.at[k],
            device_id=peer_id(peer, inner),
            device_id_type=pl.DeviceIdType.MESH,
        )

    def result_copy(peer):
        k = lax.rem(peer + peers - me, peers)
        return pltpu.make_async_remote_copy(
            src_ref=back_send.at[peer],
            dst_ref=back.at[me],
            send_sem=back_out_sem.at[k],
            recv_sem=back_in_sem.at[k],
            device_id=peer_id(peer, inner),
            device_id_type=pl.DeviceIdType.MESH,
        )

    def start(k, carry):
        input_copy(k).start()
        return carry

    lax.fori_loop(1, peers, start, 0)
    build_all(tiled, bands)

    def load_flat(chan, begin, count):
        return plane_ref[chan, pl.ds(pl.multiple_of(begin, 16), count), :]

    def emit_flat(begin, values):
        flat[pl.ds(pl.multiple_of(begin, 16), values.shape[0]), :] = values

    unet(extent, 1, load_flat, emit_flat, bands, scratch)

    def finish(k, carry):
        input_copy(k).wait()
        return carry

    lax.fori_loop(1, peers, finish, 0)

    def load_cross(chan, begin, count):
        return recv[pl.ds(begin // span, count // span), :, chan].reshape(count, extent)

    def emit_cross(begin, values):
        rows = values.shape[0] // span
        values = values.reshape(rows, 2, cut, 3 * extent)
        pieces = [
            values[:, run, :, out * extent : (out + 1) * extent]
            for run in range(2)
            for out in range(3)
        ]
        z = begin // span
        back_send[pl.ds(z, rows)] = jnp.concatenate(pieces, axis=1).astype(BF16)
        for row in range(rows):

            @pl.when(z + row != me)
            def _():
                result_copy(z + row).start()

            @pl.when(z + row == me)
            def _():
                back[pl.ds(me, 1)] = back_send[pl.ds(me, 1)]

    group = max(32, 2 * span) // span
    unet(peers, span, load_cross, emit_cross, bands, scratch, me // group + 1)

    def settle(k, carry):
        result_copy(lax.rem(me + k, peers)).wait()
        return carry

    lax.fori_loop(1, peers, settle, 0)

    def result(run, out):
        begin = (run * 3 + out) * cut
        values = back[:, begin : begin + cut, :].astype(F32).reshape(extent, extent)
        return values.T if run == 1 else values

    out_ref[0] = (result(0, 0) + result(1, 0)) * 0.5
    out_ref[1] = (flat[:, :extent] + result(1, 1)) * 0.5
    out_ref[2] = (flat[:, extent : 2 * extent] + result(0, 1)) * 0.5
    out_ref[3] = (flat[:, 2 * extent :] + result(0, 2) + result(1, 2)) / 3.0


def prepare(weights):
    w_in, w_out = weights[0], weights[6]
    tiled_in = jnp.tile(jnp.swapaxes(w_in, 1, 2).reshape(18, 32), (1, 8))
    tiled_out = jnp.tile(jnp.swapaxes(w_out, 0, 1), (8, 1))
    return [tiled_in] + list(weights[1:6]) + [tiled_out]


def shards(image, *weights):
    chan, _, extent, _ = image.shape
    peers = lax.axis_size(AXES)
    cut = extent // peers
    sems = [pltpu.SemaphoreType.DMA((peers,))] * 4
    flows = pl.pallas_call(
        functools.partial(window_kernel, peers, lax.axis_size("sub")),
        out_shape=jax.ShapeDtypeStruct((4, extent, extent), F32),
        in_specs=[pl.BlockSpec(memory_space=pltpu.VMEM)] * 8,
        out_specs=pl.BlockSpec(memory_space=pltpu.VMEM),
        scratch_shapes=BAND_SCRATCH
        + unit_scratch(peers, 2 * cut, extent)
        + [
            pltpu.VMEM((peers, 2, chan, cut, extent), F32),
            pltpu.VMEM((peers, 2, chan, cut, extent), F32),
            pltpu.VMEM((extent, 3 * extent), F32),
            pltpu.VMEM((peers, 6 * cut, extent), BF16),
            pltpu.VMEM((peers, 6 * cut, extent), BF16),
        ]
        + sems,
        compiler_params=pltpu.CompilerParams(
            vmem_limit_bytes=50 << 20, collective_id=0, has_side_effects=True
        ),
    )(image[:, 0], *prepare(weights))
    return flows[:, None]


def solution(mesh):
    split = P(None, ("groups", "slab", "sub"), None, None)
    return jax.shard_map(
        shards,
        mesh=mesh,
        in_specs=(split,) + (P(),) * 7,
        out_specs=split,
        check_vma=False,
    )
```

```python
import functools

import jax
import jax.numpy as jnp
from jax import lax
from jax.experimental import pallas as pl
from jax.experimental.pallas import tpu as pltpu
from jax.sharding import PartitionSpec as P

F32, BF16 = jnp.float32, jnp.bfloat16
BLOCKS = 16
LANES = 256
AXES = ("slab", "sub")
UNITS = 32
LAST_UNITS = 64
UNROLL = 4

BANDS = {
    "down2": (32, 64, (0, 0, 1, 1, 2, 2, 3, 3, 4, 4, -1, -1), 0.25),
    "down3": (64, 128, (0, 0, 1, 1, 2, 2, -1, -1), 0.25),
    "up3": (128, 128, (0, 1, 2, -1), 1.0),
    "up2": (64, 64, (0, 1, 2, 3, 4, -1), 1.0),
    "up1": (32, 32, (0, 1, 2, 3, 4, 5, 6, 7, 8, None, None, -1), 1.0),
}


def build_band(name, weight_ref, band_ref):
    chan, cell_lanes, cells, scale = BANDS[name]
    cell_of_lane = lax.broadcasted_iota(jnp.int32, (chan, LANES), 1) // cell_lanes
    depth = chan * len(cells)
    chan_out = weight_ref.shape[1]
    for down in range(3):
        taps = []
        for c in range(3):
            flipped = (weight_ref[3 * down + c].astype(F32) * scale).T
            taps.append(jnp.concatenate([flipped] * (LANES // chan_out), axis=1))
        for number, cell in enumerate(cells):
            total = jnp.zeros((chan, LANES), F32)
            if cell is not None:
                for c in range(3):
                    total = jnp.where(cell_of_lane == cell - c + 1, taps[c], total)
            start = down * depth + number * chan
            band_ref[start : start + chan, :] = total.astype(BF16)


def build_in(weight_ref, band_ref):
    shape = (128, LANES)
    row = lax.broadcasted_iota(jnp.int32, shape, 0)
    cell = lax.broadcasted_iota(jnp.int32, shape, 1) // 32
    for down in range(3):
        total = jnp.zeros(shape, F32)
        for c in range(3):
            flipped = weight_ref[3 * down + c].astype(F32).T
            tiled = jnp.concatenate([flipped] * 8, axis=1)
            for chan in range(2):
                here = row - 16 * chan - cell == c
                total = jnp.where(here, tiled[chan : chan + 1, :], total)
        band_ref[128 * down : 128 * down + 128, :] = total.astype(BF16)


def build_out(weight_ref, band_ref):
    shape = (LANES, 128)
    lane = lax.broadcasted_iota(jnp.int32, shape, 1)
    keep = lax.broadcasted_iota(jnp.int32, shape, 0) // 32 == lane % 8
    total = jnp.zeros(shape, F32)
    flipped = weight_ref[...].astype(F32).T
    tiled = jnp.concatenate([flipped] * 8, axis=0)
    for out in range(3):
        value = tiled[:, out : out + 1]
        total = jnp.where(keep & (lane // 32 == out), value, total)
    band_ref[...] = total.astype(BF16)


def neighbours(values):
    count = values.shape[0]
    block = lax.broadcasted_iota(jnp.int32, (count, BLOCKS, 128), 1)
    right = pltpu.roll(values[..., :128], 1, 1)
    left = pltpu.roll(values[..., 128:], BLOCKS - 1, 1)
    right = jnp.where(block == 0, 0.0, right)
    left = jnp.where(block == BLOCKS - 1, 0.0, left)
    return right, left


def narrow_halo(values):
    right, left = neighbours(values)
    lane = lax.broadcasted_iota(jnp.int32, right.shape, 2)
    return jnp.where(lane < 64, right, left)


def store_narrow(ref, start, values):
    count = values.shape[0]
    ref[pl.ds(start, count), :, :256] = values.astype(BF16)
    ref[pl.ds(start, count), :, 256:] = narrow_halo(values).astype(BF16)


def store_wide(ref, start, values):
    count = values.shape[0]
    right, left = neighbours(values)
    ref[pl.ds(start, count), :, :256] = values.astype(BF16)
    ref[pl.ds(start, count), :, 256:384] = right.astype(BF16)
    ref[pl.ds(start, count), :, 384:] = left.astype(BF16)


def conv(ref, band_ref, start, count, span):
    depth = ref.shape[2]
    parts = [ref[pl.ds(start + down * span, count)] for down in range(3)]
    rows = jnp.concatenate(parts, axis=-1).reshape(count * BLOCKS, 3 * depth)
    total = jnp.dot(rows, band_ref[...], preferred_element_type=F32)
    return jnp.maximum(total, 0.0).reshape(count, BLOCKS, LANES)


def pair_sum(values, span):
    count = values.shape[0]
    pairs = values.reshape(count // (2 * span), 2, span, BLOCKS, LANES)
    return (pairs[:, 0] + pairs[:, 1]).reshape(count // 2, BLOCKS, LANES)


def twice(values, span):
    count = values.shape[0]
    rows = values.reshape(count // span, 1, span, BLOCKS, LANES)
    return jnp.broadcast_to(rows, (count // span, 2, span, BLOCKS, LANES)).reshape(
        2 * count, BLOCKS, LANES
    )


def clear_edges(ref, height, span):
    zero = jnp.zeros((span,) + tuple(ref.shape[1:]), ref.dtype)
    ref[pl.ds(0, span)] = zero
    ref[pl.ds((height + 1) * span, span)] = zero


def chunk_units(total, span, most):
    return min(max(most, 2 * span), total)


def chunks(total, count, body, first=0):
    steps = total // count
    if steps == 1:
        body(0, count)
    else:

        def step(i, carry):
            body(lax.rem(i + first, steps) * count, count)
            return carry

        lax.fori_loop(0, steps, step, 0, unroll=min(steps, UNROLL))


def unet(height, span, load, emit, bands, scratch, first=0):
    b_in, b_down2, b_down3, b_up3, b_up2, b_up1, b_out = bands
    win, a1, p1, a2, p2, a3, s2, s1, spread = scratch
    for ref, rows in ((win, height), (p1, height // 2), (p2, height // 4), (a3, height // 4)):
        clear_edges(ref, rows, span)
    clear_edges(s2, height // 2, span)
    clear_edges(s1, height, span)
    units = height * span

    def fill(g, count):
        shape = (count, BLOCKS, 128)
        lane = lax.broadcasted_iota(jnp.int32, shape, 2)
        block = lax.broadcasted_iota(jnp.int32, shape, 1)
        outside = ((block == BLOCKS - 1) & (lane % 16 == 0)) | ((block == 0) & (lane % 16 == 9))
        rolled = []
        for chan in range(2):
            row = pltpu.roll(load(chan, g, count).astype(F32), 9 + 16 * chan, 1)
            row = jnp.broadcast_to(row[:, None, :], shape)
            rolled.append(pltpu.roll(row, 0, 2, stride=8, stride_axis=1))
        merged = jnp.where(lane < 16, rolled[0], rolled[1])
        win[pl.ds(g + span, count)] = jnp.where(outside, 0.0, merged).astype(BF16)

    chunks(units, chunk_units(units, span, 32), fill)

    def level1(g, count):
        values = conv(win, b_in, g, count, span)
        a1[pl.ds(g, count)] = values.astype(BF16)
        store_narrow(p1, g // 2 + span, pair_sum(values, span))

    chunks(units, chunk_units(units, span, UNITS), level1)

    def level2(g, count):
        values = conv(p1, b_down2, g, count, span)
        a2[pl.ds(g, count)] = values.astype(BF16)
        store_wide(p2, g // 2 + span, pair_sum(values, span))

    chunks(units // 2, chunk_units(units // 2, span, UNITS), level2)

    def level3(g, count):
        store_wide(a3, g + span, conv(p2, b_down3, g, count, span))

    chunks(units // 4, chunk_units(units // 4, span, UNITS), level3)

    def level3_up(g, count):
        values = twice(conv(a3, b_up3, g, count, span), span)
        skip = a2[pl.ds(2 * g, 2 * count)].astype(F32)
        store_narrow(s2, 2 * g + span, values + skip)

    chunks(units // 4, chunk_units(units // 4, span, UNITS), level3_up)

    def level2_up(g, count):
        values = twice(conv(s2, b_up2, g, count, span), span)
        skip = a1[pl.ds(2 * g, 2 * count)].astype(F32)
        store_narrow(s1, 2 * g + span, values + skip)

    chunks(units // 2, chunk_units(units // 2, span, UNITS), level2_up)

    def level1_up(g, count):
        values = conv(s1, b_up1, g, count, span).astype(BF16)
        spread[pl.ds(0, count * BLOCKS), :] = jnp.dot(
            values.reshape(count * BLOCKS, LANES), b_out[...], preferred_element_type=F32
        )
        lane = lax.broadcasted_iota(jnp.int32, (count, 128), 1)
        quads = []
        for quad in range(4):
            total = None
            for part in range(4):
                row = BLOCKS - 1 - (4 * quad + part)
                piece = spread[pl.ds(row, count, stride=BLOCKS), :]
                total = piece if part == 0 else jnp.where(lane % 32 // 8 == part, piece, total)
            quads.append(total)
        outs = []
        for out in range(3):
            total = None
            for quad in range(4):
                shift = 32 * (quad - out) % 128
                piece = quads[quad] if shift == 0 else pltpu.roll(quads[quad], shift, 1)
                total = piece if quad == 0 else jnp.where(lane // 32 == quad, piece, total)
            outs.append(total)
        emit(g, jnp.concatenate(outs, axis=1))

    chunks(units, chunk_units(units, span, LAST_UNITS), level1_up, first)


def unit_scratch(height, span, extent):
    def spec(rows, lanes, edge=True):
        pad = 2 if edge else 0
        flat = extent * rows // height + pad
        return pltpu.VMEM((max((rows + pad) * span, flat), BLOCKS, lanes), BF16)

    return [
        spec(height, 128),
        spec(height, 256, False),
        spec(height // 2, 384),
        spec(height // 2, 256, False),
        spec(height // 4, 512),
        spec(height // 4, 512),
        spec(height // 2, 384),
        spec(height, 384),
        pltpu.VMEM((max(LAST_UNITS, 2 * span) * BLOCKS, 128), F32),
    ]


BAND_SCRATCH = [
    pltpu.VMEM((384, 256), BF16),
    pltpu.VMEM((1152, 256), BF16),
    pltpu.VMEM((1536, 256), BF16),
    pltpu.VMEM((1536, 256), BF16),
    pltpu.VMEM((1152, 256), BF16),
    pltpu.VMEM((1152, 256), BF16),
    pltpu.VMEM((256, 128), BF16),
]


def build_all(tiled, bands):
    build_in(tiled[0], bands[0])
    for name, source, band in zip(("down2", "down3", "up3", "up2", "up1"), tiled[1:6], bands[1:6]):
        build_band(name, source, band)
    build_out(tiled[6], bands[6])


def peer_id(index, inner):
    return {"slab": index // inner, "sub": lax.rem(index, inner)}


def window_kernel(peers, inner, image_ref, *refs):
    given, out_ref, bands = refs[:7], refs[7], refs[8:15]
    scratch = refs[15:24]
    send, recv, flat, back_send, back, out_sem, in_sem, back_out_sem, back_in_sem = refs[24:33]
    plane_ref, weights, local_sem = refs[33], refs[34:41], refs[41]
    copies = [pltpu.make_async_copy(image_ref.at[:, 0], plane_ref, local_sem.at[0])]
    for number in range(7):
        copies.append(
            pltpu.make_async_copy(given[number], weights[number], local_sem.at[1 + number])
        )
    for copy in copies:
        copy.start()
    extent = plane_ref.shape[1]
    cut = extent // peers
    span = 2 * cut
    me = lax.axis_index("slab") * inner + lax.axis_index("sub")

    barrier = pltpu.get_barrier_semaphore()

    def greet(k, carry):
        pl.semaphore_signal(
            barrier,
            inc=1,
            device_id=peer_id(lax.rem(me + k, peers), inner),
            device_id_type=pl.DeviceIdType.MESH,
        )
        return carry

    lax.fori_loop(1, peers, greet, 0)
    copies[0].wait()
    for chan in range(2):
        plane = plane_ref[chan].astype(F32)
        send[:, 0, chan] = plane.reshape(peers, cut, extent)
        send[:, 1, chan] = plane.T.reshape(peers, cut, extent)
    recv[pl.ds(me, 1)] = send[pl.ds(me, 1)]
    pl.semaphore_wait(barrier, peers - 1)

    def input_copy(k):
        peer = lax.rem(me + k, peers)
        return pltpu.make_async_remote_copy(
            src_ref=send.at[peer],
            dst_ref=recv.at[me],
            send_sem=out_sem.at[k],
            recv_sem=in_sem.at[k],
            device_id=peer_id(peer, inner),
            device_id_type=pl.DeviceIdType.MESH,
        )

    def result_copy(peer):
        k = lax.rem(peer + peers - me, peers)
        return pltpu.make_async_remote_copy(
            src_ref=back_send.at[peer],
            dst_ref=back.at[me],
            send_sem=back_out_sem.at[k],
            recv_sem=back_in_sem.at[k],
            device_id=peer_id(peer, inner),
            device_id_type=pl.DeviceIdType.MESH,
        )

    def start(k, carry):
        input_copy(k).start()
        return carry

    lax.fori_loop(1, peers, start, 0)
    for copy in copies[1:]:
        copy.wait()
    build_all(weights, bands)

    def load_flat(chan, begin, count):
        return plane_ref[chan, pl.ds(pl.multiple_of(begin, 16), count), :]

    def emit_flat(begin, values):
        flat[pl.ds(pl.multiple_of(begin, 16), values.shape[0]), :] = values

    unet(extent, 1, load_flat, emit_flat, bands, scratch)

    def finish(k, carry):
        input_copy(k).wait()
        return carry

    lax.fori_loop(1, peers, finish, 0)

    def load_cross(chan, begin, count):
        return recv[pl.ds(begin // span, count // span), :, chan].reshape(count, extent)

    def emit_cross(begin, values):
        rows = values.shape[0] // span
        values = values.reshape(rows, 2, cut, 3 * extent)
        pieces = [
            values[:, run, :, out * extent : (out + 1) * extent]
            for run in range(2)
            for out in range(3)
        ]
        z = begin // span
        back_send[pl.ds(z, rows)] = jnp.concatenate(pieces, axis=1).astype(BF16)
        for row in range(rows):

            @pl.when(z + row != me)
            def _():
                result_copy(z + row).start()

            @pl.when(z + row == me)
            def _():
                back[pl.ds(me, 1)] = back_send[pl.ds(me, 1)]

    group = chunk_units(peers * span, span, LAST_UNITS) // span
    unet(peers, span, load_cross, emit_cross, bands, scratch, me // group + 1)

    def settle(k, carry):
        result_copy(lax.rem(me + k, peers)).wait()
        return carry

    lax.fori_loop(1, peers, settle, 0)

    def result(run, out):
        begin = (run * 3 + out) * cut
        values = back[:, begin : begin + cut, :].astype(F32).reshape(extent, extent)
        return values.T if run == 1 else values

    out_ref[0] = (result(0, 0) + result(1, 0)) * 0.5
    out_ref[1] = (flat[:, :extent] + result(1, 1)) * 0.5
    out_ref[2] = (flat[:, extent : 2 * extent] + result(0, 1)) * 0.5
    out_ref[3] = (flat[:, 2 * extent :] + result(0, 2) + result(1, 2)) / 3.0


def shards(image, *weights):
    chan, _, extent, _ = image.shape
    peers = lax.axis_size(AXES)
    cut = extent // peers
    sems = [pltpu.SemaphoreType.DMA((peers,))] * 4
    flows = pl.pallas_call(
        functools.partial(window_kernel, peers, lax.axis_size("sub")),
        out_shape=jax.ShapeDtypeStruct((4, extent, extent), F32),
        in_specs=[pl.BlockSpec(memory_space=pl.ANY)] * 8,
        out_specs=pl.BlockSpec(memory_space=pltpu.VMEM),
        scratch_shapes=BAND_SCRATCH
        + unit_scratch(peers, 2 * cut, extent)
        + [
            pltpu.VMEM((peers, 2, chan, cut, extent), F32),
            pltpu.VMEM((peers, 2, chan, cut, extent), F32),
            pltpu.VMEM((extent, 3 * extent), F32),
            pltpu.VMEM((peers, 6 * cut, extent), BF16),
            pltpu.VMEM((peers, 6 * cut, extent), BF16),
        ]
        + sems
        + [pltpu.VMEM((chan, extent, extent), BF16)]
        + [pltpu.VMEM(weight.shape, BF16) for weight in weights]
        + [pltpu.SemaphoreType.DMA((8,))],
        compiler_params=pltpu.CompilerParams(
            vmem_limit_bytes=50 << 20, collective_id=0, has_side_effects=True
        ),
    )(image, *weights)
    return flows[:, None]


def solution(mesh):
    split = P(None, ("groups", "slab", "sub"), None, None)
    return jax.shard_map(
        shards,
        mesh=mesh,
        in_specs=(split,) + (P(),) * 7,
        out_specs=split,
        check_vma=False,
    )
```
